32 devices in a mesh: dp: 4 (over y, core), seq: 4 (over z), tensor: 2 (over x).
Axes of the slice: x: 2, y: 2, z: 4, core: 2. Of those that a mesh axis runs over, the one named last changes fastest.
Arguments:
- tokens: bfloat16 [8192, 2048], P(('dp', 'seq')), may hold values from -6 to 6
- out_grad: bfloat16 [8192, 2048], P(('dp', 'seq')), may hold values from -6 to 6
- positions: int32 [4, 2048], P('dp'), may hold values from 0 to 1151, as said below
- attn_gain: float32 [2048], P(('dp', 'seq')), may hold values from 0.5 to 1.5
- q_weight: float32 [2048, 2048], P(('dp', 'seq'), 'tensor'), may hold values from -0.125 to 0.125
- k_weight: float32 [2048, 512], P(('dp', 'seq'), 'tensor'), may hold values from -0.125 to 0.125
- v_weight: float32 [2048, 512], P(('dp', 'seq'), 'tensor'), may hold values from -0.125 to 0.125
- o_weight: float32 [2048, 2048], P(('dp', 'seq'), 'tensor'), may hold values from -1.5 to 1.5
- mlp_gain: float32 [2048], P(('dp', 'seq')), may hold values from 0.5 to 1.5
- gate_weight: float32 [2048, 8192], P(('dp', 'seq'), 'tensor'), may hold values from -0.125 to 0.125
- up_weight: float32 [2048, 8192], P(('dp', 'seq'), 'tensor'), may hold values from -0.125 to 0.125
- down_weight: float32 [2048, 8192], P(('dp', 'seq'), 'tensor'), may hold values from -0.0625 to 0.0625
Outputs:
- output: bfloat16 [8192, 2048], P(('dp', 'seq'))
- tokens_grad: bfloat16 [8192, 2048], P(('dp', 'seq'))
- attn_gain_grad: float32 [2048], P(('dp', 'seq'))
- q_weight_grad: float32 [2048, 2048], P(('dp', 'seq'), 'tensor')
- k_weight_grad: float32 [2048, 512], P(('dp', 'seq'), 'tensor')
- v_weight_grad: float32 [2048, 512], P(('dp', 'seq'), 'tensor')
- o_weight_grad: float32 [2048, 2048], P(('dp', 'seq'), 'tensor')
- mlp_gain_grad: float32 [2048], P(('dp', 'seq'))
- gate_weight_grad: float32 [2048, 8192], P(('dp', 'seq'), 'tensor')
- up_weight_grad: float32 [2048, 8192], P(('dp', 'seq'), 'tensor')
- down_weight_grad: float32 [2048, 8192], P(('dp', 'seq'), 'tensor')
The draws below stay inside these ranges and needn't reach their ends.
Inputs may be any that keep to these rules, and one draw needn't show every extreme that they name: In each group, every block of 512 rows (aligned) holds 256 prompt tokens followed by 2 whole continuations of 128 rows; the prompt's positions 0 to 1023 each occur once in the group, in a drawn order; a continuation's rows hold positions 1024 to 1151 in order.
All inputs are finite; a program needn't handle non-finite values.
Results may differ from the reference program's by a relative error of at most 0.018.
Values may be sent and summed in bfloat16 or wider, within the bound.
A program may use at most 384 MiB of HBM per device.

```python
import math
import jax
import jax.numpy as jnp
import numpy as np
from jax import lax

D = 2048
HEADS = 32
KV_HEADS = 8
HEAD_DIM = 64
FF = 8192
PROMPT = 1024
CONT_LEN = 128
QW = 2048
KW = 512
GROUP_LEN = 2048
GROUPS = 4
TOKENS = 8192
TOK_DEV = 512
PROMPT_DEV = 256
CONT_DEV = 2


def layout(key):
    group_keys = jax.random.split(jax.random.fold_in(key, 11), GROUPS)

    def one_group(group_key):
        block_count = PROMPT // PROMPT_DEV
        prompt_order = jax.random.permutation(group_key, PROMPT).astype(jnp.int32).reshape(block_count, PROMPT_DEV)
        cont_pos = jnp.tile(PROMPT + jnp.arange(CONT_LEN, dtype=jnp.int32), (block_count, CONT_DEV))
        return jnp.concatenate([prompt_order, cont_pos], axis=1).reshape(-1)
    return jax.vmap(one_group)(group_keys)


def draw_positions(key, part):
    return layout(key)


def steps_of(rng, extent, cuts, least, high):
    level = 1.0
    for dim, blocks in cuts:
        draws = jax.random.uniform(jax.random.fold_in(jax.random.fold_in(rng, 6), dim), (blocks,), jnp.float32, least / len(cuts), high / len(cuts))
        level = level * jnp.repeat(jnp.exp(draws), extent[dim] // blocks).reshape((-1,) + (1,) * (len(extent) - 1 - dim))
    return level


def normal_values(key, shape, width, limit, pieces=(), held_as=jnp.bfloat16):
    factor_of = steps_of(key, shape, pieces, -0.22, 0.18) if pieces else 1.0
    entries = jax.random.normal(key, shape, jnp.float32) * width * factor_of
    return jnp.minimum(jnp.maximum(entries, -limit), limit).astype(held_as)


def setup_inputs(seed: int = 0) -> dict:
    arg_keys = jax.random.split(jax.random.key(seed), 13)
    tokens = normal_values(arg_keys[0], (TOKENS, D), 1.0, 6.0, ((0, 16),))
    out_grad = normal_values(arg_keys[1], (TOKENS, D), 1.0, 6.0, ((0, 16),))
    positions = draw_positions(jax.random.fold_in(arg_keys[12], 71), 0)
    attn_gain = jnp.clip(1.0 + 0.1 * jax.random.normal(arg_keys[3], (D,), jnp.float32), 0.5, 1.5)
    q_weight = normal_values(arg_keys[4], (D, QW), D ** -0.5, 0.125, ((0, 16), (1, 2)), jnp.float32)
    k_weight = normal_values(arg_keys[5], (D, KW), D ** -0.5, 0.125, ((0, 16), (1, 2)), jnp.float32)
    v_weight = normal_values(arg_keys[6], (D, KW), D ** -0.5, 0.125, ((0, 16), (1, 2)), jnp.float32)
    o_weight = normal_values(arg_keys[7], (D, QW), (max(QW // 128, 4)) ** -0.5, 1.5, ((0, 16), (1, 2)), jnp.float32)
    mlp_gain = jnp.clip(1.0 + 0.1 * jax.random.normal(arg_keys[8], (D,), jnp.float32), 0.5, 1.5)
    gate_weight = normal_values(arg_keys[9], (D, FF), D ** -0.5, 0.125, ((0, 16), (1, 2)), jnp.float32)
    up_weight = normal_values(arg_keys[10], (D, FF), D ** -0.5, 0.125, ((0, 16), (1, 2)), jnp.float32)
    down_weight = normal_values(arg_keys[11], (D, FF), FF ** -0.5, 0.0625, ((0, 16), (1, 2)), jnp.float32)
    return {"tokens": tokens, "out_grad": out_grad, "positions": positions, "attn_gain": attn_gain, "q_weight": q_weight, "k_weight": k_weight, "v_weight": v_weight, "o_weight": o_weight, "mlp_gain": mlp_gain, "gate_weight": gate_weight, "up_weight": up_weight, "down_weight": down_weight}


epsilon = 1e-05
highest = lax.Precision.HIGHEST

@jax.custom_vjp
def low(v):
    return lax.optimization_barrier(v.astype(jnp.bfloat16)).astype(jnp.float32)

@jax.custom_vjp
def low_back(v):
    return v

def low_keep(v):
    return (low(v), None)

def low_pass(kept, grad):
    return (grad,)

def back_keep(v):
    return (v, None)

def back_low(kept, grad):
    return (low(grad),)
low.defvjp(low_keep, low_pass)
low_back.defvjp(back_keep, back_low)

def rope_freqs(head_width):
    scaled_list = []
    for column in range(head_width // 2):
        inverse = 1.0 / 500000.0 ** (2.0 * column / head_width)
        wavelength = 2.0 * math.pi / inverse
        if wavelength < 2048.0:
            scaled_list.append(inverse)
        elif wavelength > 8192.0:
            scaled_list.append(inverse / 32.0)
        else:
            smooth_mix = (8192.0 / wavelength - 1.0) / 3.0
            scaled_list.append((1.0 - smooth_mix) * inverse / 32.0 + smooth_mix * inverse)
    return np.array(scaled_list, dtype=np.float32)

def rope_apply(values, cos_table, sin_table):
    half_width = values.shape[-1] // 2
    turned = jnp.concatenate([-values[..., half_width:], values[..., :half_width]], axis=-1)
    return values * cos_table + turned * sin_table

def rms_norm(values, gain_vec):
    inv_rms = lax.rsqrt(lax.optimization_barrier(jnp.mean(values * values, axis=-1, keepdims=True)) + epsilon)
    return values * inv_rms * gain_vec

def matmul(left_side, right_side):
    return jnp.dot(left_side, right_side, precision=highest, preferred_element_type=jnp.float32)

def group_segments():
    row_index = jnp.arange(GROUP_LEN, dtype=jnp.int32)
    offset = row_index % TOK_DEV
    block_index = row_index // TOK_DEV
    cont_number = 1 + block_index * CONT_DEV + (offset - PROMPT_DEV) // CONT_LEN
    return jnp.where(offset < PROMPT_DEV, jnp.zeros_like(offset), cont_number).astype(jnp.int32)

def group_forward(params, inputs, positions, segments):
    attn_gain, q_weight, k_weight, v_weight, o_weight, mlp_gain, gate_weight, up_weight, down_weight = params
    length = inputs.shape[0]
    normed = low(rms_norm(inputs, low(attn_gain)))
    angles = positions.astype(jnp.float32)[:, None] * jnp.asarray(rope_freqs(HEAD_DIM), jnp.float32)[None, :]
    angles = jnp.concatenate([angles, angles], axis=1)
    cos_table = jnp.cos(angles)[:, None, :]
    sin_table = jnp.sin(angles)[:, None, :]
    query_raw = low_back(matmul(normed, low(q_weight)))
    key_raw = low_back(matmul(normed, low(k_weight)))
    value_all = low(low_back(matmul(normed, low(v_weight))))
    queries = low(rope_apply(query_raw.reshape(length, HEADS, HEAD_DIM), cos_table, sin_table))
    key_all = low(rope_apply(key_raw.reshape(length, KV_HEADS, HEAD_DIM), cos_table, sin_table))
    values = value_all.reshape(length, KV_HEADS, HEAD_DIM)
    group_size = HEADS // KV_HEADS
    block_rows = math.gcd(length, 512)
    blocks = length // block_rows
    score_scale = 1.0 / math.sqrt(HEAD_DIM)

    def attend_block(block_item):
        query_block, query_pos, query_seg = block_item
        query_block = query_block.reshape(block_rows, KV_HEADS, group_size, HEAD_DIM)
        scores = jnp.einsum('qkgd,ckd->kgqc', query_block, key_all, precision=highest) * score_scale
        scores = low_back(scores)
        visible = (positions[None, :] <= query_pos[:, None]) & ((segments[None, :] == 0) | (segments[None, :] == query_seg[:, None]))
        scores = jnp.where(visible[None, None], scores, -1e+30)
        row_max = lax.optimization_barrier(jnp.max(scores, axis=-1, keepdims=True))
        exponent = jnp.exp(scores - row_max)
        probability = exponent / lax.optimization_barrier(jnp.sum(exponent, axis=-1, keepdims=True))
        mixed_rows = jnp.einsum('kgqc,ckd->qkgd', low(probability), values, precision=highest)
        return mixed_rows.reshape(block_rows, QW)
    attended = lax.map(jax.checkpoint(attend_block), (queries.reshape(blocks, block_rows, HEADS, HEAD_DIM), positions.reshape(blocks, block_rows), segments.reshape(blocks, block_rows)))
    attended = low(low_back(attended.reshape(length, QW)))
    middle = inputs + low_back(matmul(attended, low(o_weight).T))
    normed_two = low(rms_norm(middle, low(mlp_gain)))
    gate_pre = low_back(matmul(normed_two, low(gate_weight)))
    upward = low_back(matmul(normed_two, low(up_weight)))
    hidden = low(jax.nn.silu(gate_pre) * upward)
    return middle + low_back(matmul(hidden, low(down_weight).T))

def reference(tokens, out_grad, positions, attn_gain, q_weight, k_weight, v_weight, o_weight, mlp_gain, gate_weight, up_weight, down_weight):
    params = (attn_gain, q_weight, k_weight, v_weight, o_weight, mlp_gain, gate_weight, up_weight, down_weight)
    inputs = tokens.astype(jnp.float32).reshape(GROUPS, GROUP_LEN, D)
    cotangent = out_grad.astype(jnp.float32).reshape(GROUPS, GROUP_LEN, D)
    segments = group_segments()

    def one_group(totals, block_item):
        group_in, group_cot, group_pos = block_item

        def forward(weights, values):
            return group_forward(weights, values, group_pos, segments)
        result, pullback = jax.vjp(forward, params, group_in)
        weight_grads, input_grad = pullback(group_cot)
        totals = tuple((total_part + new_part for total_part, new_part in zip(totals, weight_grads)))
        return (totals, (result.astype(jnp.bfloat16), input_grad.astype(jnp.bfloat16)))
    zero_grads = tuple((jnp.zeros_like(param_item) for param_item in params))
    totals, (results, input_grads) = lax.scan(one_group, zero_grads, (inputs, cotangent, positions))
    return (results.reshape(TOKENS, D), input_grads.reshape(TOKENS, D), totals[0], totals[1], totals[2], totals[3], totals[4], totals[5], totals[6], totals[7], totals[8])
```

```python
import math

import jax
import jax.numpy as jnp
import numpy as np
from jax import lax
from jax.sharding import PartitionSpec as P

HEAD_DIM = 64
PROMPT = 1024
CONT_LEN = 128


epsilon = 1e-05


def for_sending(array):
    return jax.tree.map(lambda a: a.astype(jnp.bfloat16) if a.dtype == jnp.float32 else a, array)


def rope_freqs(head_width):
    scaled_list = []
    for column in range(head_width // 2):
        inverse = 1.0 / 500000.0 ** (2.0 * column / head_width)
        wavelength = 2.0 * math.pi / inverse
        if wavelength < 2048.0:
            scaled_list.append(inverse)
        elif wavelength > 8192.0:
            scaled_list.append(inverse / 32.0)
        else:
            smooth_mix = (8192.0 / wavelength - 1.0) / 3.0
            scaled_list.append((1.0 - smooth_mix) * inverse / 32.0 + smooth_mix * inverse)
    return np.array(scaled_list, dtype=np.float32)


def rope_apply(values, cos_table, sin_table):
    half_width = values.shape[-1] // 2
    turned = jnp.concatenate([-values[..., half_width:], values[..., :half_width]], axis=-1)
    return values * cos_table + turned * sin_table


def rope_back(grads, cos_table, sin_table):
    half_width = grads.shape[-1] // 2
    twisted = grads * sin_table
    return grads * cos_table + jnp.concatenate(
        [twisted[..., half_width:], -twisted[..., :half_width]], axis=-1
    )


def norm_parts(values):
    inv_rms = lax.rsqrt(jnp.mean(values * values, axis=-1, keepdims=True) + epsilon)
    return (values * inv_rms, inv_rms)


def norm_back(grad_normed, unit_rows, inv_rms, gain_vec):
    grad_unit = grad_normed * gain_vec
    return inv_rms * (
        grad_unit - unit_rows * jnp.mean(grad_unit * unit_rows, axis=-1, keepdims=True)
    )


def times_transposed(left_side, right_side):
    return lax.dot_general(
        left_side, right_side, (((1,), (1,)), ((), ())), preferred_element_type=jnp.float32
    )


def transposed_times(left_side, right_side):
    return lax.dot_general(
        left_side, right_side, (((0,), (0,)), ((), ())), preferred_element_type=jnp.float32
    )


def local(
    tokens,
    out_grad,
    positions,
    attn_gain,
    q_weight,
    k_weight,
    v_weight,
    o_weight,
    mlp_gain,
    gate_weight,
    up_weight,
    down_weight,
):
    seq_count = lax.axis_size("seq")
    seq_rank = lax.axis_index("seq")
    tok_rows = tokens.shape[0]
    prompt_rows = PROMPT // seq_count
    cont_here = (tok_rows - prompt_rows) // CONT_LEN
    all_pos = positions[0]
    own_pos = lax.dynamic_slice_in_dim(all_pos, seq_rank * tok_rows, tok_rows)
    row_offset = jnp.arange(tok_rows, dtype=jnp.int32)
    cont_number = 1 + seq_rank * cont_here + (row_offset - prompt_rows) // CONT_LEN
    own_seg = jnp.where(row_offset < prompt_rows, jnp.zeros_like(row_offset), cont_number)
    prompt_pos = all_pos.reshape(seq_count, tok_rows)[:, :prompt_rows].reshape(-1)
    key_pos = jnp.concatenate([prompt_pos, own_pos[prompt_rows:]])
    key_seg = jnp.concatenate([jnp.zeros_like(prompt_pos), own_seg[prompt_rows:]])
    visible = (key_pos[None, :] <= own_pos[:, None]) & (
        (key_seg[None, :] == 0) | (key_seg[None, :] == own_seg[:, None])
    )
    prompt_count = prompt_pos.shape[0]
    angles = (
        own_pos.astype(jnp.float32)[:, None]
        * jnp.asarray(rope_freqs(HEAD_DIM), jnp.float32)[None, :]
    )
    angles = jnp.concatenate([angles, angles], axis=1)
    cos_table = jnp.cos(angles)[:, None, :]
    sin_table = jnp.sin(angles)[:, None, :]
    score_scale = 1.0 / math.sqrt(HEAD_DIM)

    def attn_pack():
        return (
            attn_gain.astype(jnp.bfloat16),
            q_weight.astype(jnp.bfloat16),
            k_weight.astype(jnp.bfloat16),
            v_weight.astype(jnp.bfloat16),
            o_weight.astype(jnp.bfloat16),
        )

    def mlp_pack():
        return (
            mlp_gain.astype(jnp.bfloat16),
            gate_weight.astype(jnp.bfloat16),
            up_weight.astype(jnp.bfloat16),
            down_weight.astype(jnp.bfloat16),
        )

    attn_set = lax.all_gather(for_sending(attn_pack()), ("dp", "seq"), axis=0, tiled=True)
    mlp_set = lax.all_gather(for_sending(mlp_pack()), ("dp", "seq"), axis=0, tiled=True)
    inputs = tokens.astype(jnp.float32)
    unit_one, rms_one = norm_parts(inputs)
    normed = (unit_one * attn_set[0].astype(jnp.float32)).astype(jnp.bfloat16)
    query_raw = jnp.dot(normed, attn_set[1], preferred_element_type=jnp.float32)
    key_raw = jnp.dot(normed, attn_set[2], preferred_element_type=jnp.float32)
    value_raw = jnp.dot(normed, attn_set[3], preferred_element_type=jnp.float32)
    local_heads = query_raw.shape[1] // HEAD_DIM
    local_kv = key_raw.shape[1] // HEAD_DIM
    group_size = local_heads // local_kv
    queries = rope_apply(
        query_raw.reshape(tok_rows, local_heads, HEAD_DIM), cos_table, sin_table
    ).astype(jnp.bfloat16)
    keys_own = (
        rope_apply(key_raw.reshape(tok_rows, local_kv, HEAD_DIM), cos_table, sin_table)
        .astype(jnp.bfloat16)
        .reshape(tok_rows, -1)
    )
    values_own = value_raw.astype(jnp.bfloat16)
    prompt_keys, prompt_values = (
        lax.all_gather(keys_own[:prompt_rows], "seq", axis=0, tiled=True),
        lax.all_gather(values_own[:prompt_rows], "seq", axis=0, tiled=True),
    )
    key_all = jnp.concatenate([prompt_keys, keys_own[prompt_rows:]], axis=0).reshape(
        -1, local_kv, HEAD_DIM
    )
    value_all = jnp.concatenate([prompt_values, values_own[prompt_rows:]], axis=0).reshape(
        -1, local_kv, HEAD_DIM
    )

    def head_scores(query_group, key_group):
        scores = (
            jnp.einsum("tgd,cd->gtc", query_group, key_group, preferred_element_type=jnp.float32)
            * score_scale
        )
        return jnp.where(visible[None], scores, -1e30)

    mixed_list = []
    log_totals = []
    for kv_head in range(local_kv):
        query_group = queries[:, kv_head * group_size : (kv_head + 1) * group_size, :]
        scores = head_scores(query_group, key_all[:, kv_head, :])
        row_max = jnp.max(scores, axis=-1, keepdims=True)
        exponent = jnp.exp(scores - row_max)
        row_total = jnp.sum(exponent, axis=-1, keepdims=True)
        probability = exponent / row_total
        log_totals.append(row_max + jnp.log(row_total))
        mixed_list.append(
            jnp.einsum(
                "gtc,cd->tgd",
                probability.astype(jnp.bfloat16),
                value_all[:, kv_head, :],
                preferred_element_type=jnp.float32,
            )
        )
    attended = jnp.concatenate(mixed_list, axis=1).reshape(tok_rows, -1).astype(jnp.bfloat16)
    middle = inputs + lax.psum(
        times_transposed(attended, attn_set[4]).astype(jnp.bfloat16), "tensor"
    ).astype(jnp.float32)
    unit_two, rms_two = norm_parts(middle)
    normed_two = (unit_two * mlp_set[0].astype(jnp.float32)).astype(jnp.bfloat16)
    gate_pre = jnp.dot(normed_two, mlp_set[1], preferred_element_type=jnp.float32)
    upward = jnp.dot(normed_two, mlp_set[2], preferred_element_type=jnp.float32)
    sigmoid_gate = jax.nn.sigmoid(gate_pre)
    activated = gate_pre * sigmoid_gate
    hidden = (activated * upward).astype(jnp.bfloat16)
    result = middle + lax.psum(
        times_transposed(hidden, mlp_set[3]).astype(jnp.bfloat16), "tensor"
    ).astype(jnp.float32)
    output = result.astype(jnp.bfloat16)
    grad_out = out_grad.astype(jnp.float32)
    grad_hidden = jnp.dot(out_grad, mlp_set[3], preferred_element_type=jnp.float32)
    grad_gate = (
        grad_hidden * upward * sigmoid_gate * (1.0 + gate_pre * (1.0 - sigmoid_gate))
    ).astype(jnp.bfloat16)
    grad_up = (grad_hidden * activated).astype(jnp.bfloat16)
    grad_normed_two = lax.psum(
        (times_transposed(grad_gate, mlp_set[1]) + times_transposed(grad_up, mlp_set[2])).astype(
            jnp.bfloat16
        ),
        "tensor",
    ).astype(jnp.float32)
    gain_two_grad = jnp.sum(grad_normed_two * unit_two, axis=0)
    grad_middle = grad_out + norm_back(
        grad_normed_two, unit_two, rms_two, mlp_set[0].astype(jnp.float32)
    )
    def summed(term):
        return lax.psum_scatter(
            term.astype(jnp.bfloat16), ("dp", "seq"), scatter_dimension=0, tiled=True
        ).astype(jnp.float32)

    down_grad = summed(transposed_times(out_grad, hidden))
    gate_grad = summed(transposed_times(normed_two, grad_gate))
    up_grad = summed(transposed_times(normed_two, grad_up))
    grad_branch = grad_middle.astype(jnp.bfloat16)
    grad_attended = (
        jnp.dot(grad_branch, attn_set[4], preferred_element_type=jnp.float32)
        .astype(jnp.bfloat16)
        .reshape(tok_rows, local_heads, HEAD_DIM)
    )
    query_grads = []
    key_grads = []
    value_grads = []
    for kv_head in range(local_kv):
        query_group = queries[:, kv_head * group_size : (kv_head + 1) * group_size, :]
        key_group = key_all[:, kv_head, :]
        value_group = value_all[:, kv_head, :]
        grad_group = grad_attended[:, kv_head * group_size : (kv_head + 1) * group_size, :]
        probability = jnp.exp(head_scores(query_group, key_group) - log_totals[kv_head])
        grad_prob = jnp.einsum(
            "tgd,cd->gtc", grad_group, value_group, preferred_element_type=jnp.float32
        )
        row_dot = jnp.sum(probability * grad_prob, axis=-1, keepdims=True)
        grad_scores = (probability * (grad_prob - row_dot)).astype(jnp.bfloat16)
        query_grads.append(
            jnp.einsum("gtc,cd->tgd", grad_scores, key_group, preferred_element_type=jnp.float32)
            * score_scale
        )
        key_grads.append(
            jnp.einsum("gtc,tgd->cd", grad_scores, query_group, preferred_element_type=jnp.float32)
            * score_scale
        )
        value_grads.append(
            jnp.einsum(
                "gtc,tgd->cd",
                probability.astype(jnp.bfloat16),
                grad_group,
                preferred_element_type=jnp.float32,
            )
        )
    grad_queries = jnp.concatenate(query_grads, axis=1)
    grad_keys = jnp.stack(key_grads, axis=1).reshape(-1, local_kv * HEAD_DIM)
    grad_values = jnp.stack(value_grads, axis=1).reshape(-1, local_kv * HEAD_DIM)
    key_share, value_share = (
        lax.psum_scatter(
            grad_keys[:prompt_count].astype(jnp.bfloat16), "seq", scatter_dimension=0, tiled=True
        ).astype(jnp.float32),
        lax.psum_scatter(
            grad_values[:prompt_count].astype(jnp.bfloat16), "seq", scatter_dimension=0, tiled=True
        ).astype(jnp.float32),
    )
    grad_key_own = jnp.concatenate([key_share, grad_keys[prompt_count:]], axis=0).reshape(
        tok_rows, local_kv, HEAD_DIM
    )
    grad_query_raw = (
        rope_back(grad_queries, cos_table, sin_table).reshape(tok_rows, -1).astype(jnp.bfloat16)
    )
    grad_key_raw = (
        rope_back(grad_key_own, cos_table, sin_table).reshape(tok_rows, -1).astype(jnp.bfloat16)
    )
    grad_value_raw = jnp.concatenate([value_share, grad_values[prompt_count:]], axis=0).astype(
        jnp.bfloat16
    )
    grad_normed = lax.psum(
        (
            times_transposed(grad_query_raw, attn_set[1])
            + times_transposed(grad_key_raw, attn_set[2])
            + times_transposed(grad_value_raw, attn_set[3])
        ).astype(jnp.bfloat16),
        "tensor",
    ).astype(jnp.float32)
    gain_one_grad = jnp.sum(grad_normed * unit_one, axis=0)
    grad_inputs = grad_middle + norm_back(
        grad_normed, unit_one, rms_one, attn_set[0].astype(jnp.float32)
    )
    attn_terms = (
        gain_one_grad,
        transposed_times(normed, grad_query_raw),
        transposed_times(normed, grad_key_raw),
        transposed_times(normed, grad_value_raw),
        transposed_times(grad_branch, attended),
        gain_two_grad,
    )
    attn_grads = (
        lax.psum_scatter(attn_terms[0], ("dp", "seq"), scatter_dimension=0, tiled=True),
        summed(attn_terms[1]),
        summed(attn_terms[2]),
        summed(attn_terms[3]),
        summed(attn_terms[4]),
        lax.psum_scatter(attn_terms[5], ("dp", "seq"), scatter_dimension=0, tiled=True),
    )
    return (
        output,
        grad_inputs.astype(jnp.bfloat16),
        attn_grads[0],
        attn_grads[1],
        attn_grads[2],
        attn_grads[3],
        attn_grads[4],
        attn_grads[5],
        gate_grad,
        up_grad,
        down_grad,
    )


def solution(mesh):
    placed = (
        P(("dp", "seq"), None),
        P(("dp", "seq"), None),
        P("dp", None),
        P(("dp", "seq")),
        P(("dp", "seq"), "tensor"),
        P(("dp", "seq"), "tensor"),
        P(("dp", "seq"), "tensor"),
        P(("dp", "seq"), "tensor"),
        P(("dp", "seq")),
        P(("dp", "seq"), "tensor"),
        P(("dp", "seq"), "tensor"),
        P(("dp", "seq"), "tensor"),
    )
    return jax.shard_map(
        local,
        mesh=mesh,
        in_specs=placed,
        out_specs=(
            P(("dp", "seq"), None),
            P(("dp", "seq"), None),
            P(("dp", "seq")),
            P(("dp", "seq"), "tensor"),
            P(("dp", "seq"), "tensor"),
            P(("dp", "seq"), "tensor"),
            P(("dp", "seq"), "tensor"),
            P(("dp", "seq")),
            P(("dp", "seq"), "tensor"),
            P(("dp", "seq"), "tensor"),
            P(("dp", "seq"), "tensor"),
        ),
        check_vma=False,
    )
```

```python
import math

import jax
import jax.numpy as jnp
import numpy as np
from jax import lax
from jax.sharding import PartitionSpec as P

HEAD_DIM = 64
PROMPT = 1024
CONT_LEN = 128


epsilon = 1e-05


def rope_freqs(head_width):
    scaled_list = []
    for column in range(head_width // 2):
        inverse = 1.0 / 500000.0 ** (2.0 * column / head_width)
        wavelength = 2.0 * math.pi / inverse
        if wavelength < 2048.0:
            scaled_list.append(inverse)
        elif wavelength > 8192.0:
            scaled_list.append(inverse / 32.0)
        else:
            smooth_mix = (8192.0 / wavelength - 1.0) / 3.0
            scaled_list.append((1.0 - smooth_mix) * inverse / 32.0 + smooth_mix * inverse)
    return np.array(scaled_list, dtype=np.float32)


def rope_apply(values, cos_table, sin_table):
    half_width = values.shape[-1] // 2
    turned = jnp.concatenate([-values[..., half_width:], values[..., :half_width]], axis=-1)
    return values * cos_table + turned * sin_table


def rope_back(grads, cos_table, sin_table):
    half_width = grads.shape[-1] // 2
    twisted = grads * sin_table
    return grads * cos_table + jnp.concatenate(
        [twisted[..., half_width:], -twisted[..., :half_width]], axis=-1
    )


def norm_parts(values):
    inv_rms = lax.rsqrt(jnp.mean(values * values, axis=-1, keepdims=True) + epsilon)
    return (values * inv_rms, inv_rms)


def norm_back(grad_normed, unit_rows, inv_rms, gain_vec):
    grad_unit = grad_normed * gain_vec
    return inv_rms * (
        grad_unit - unit_rows * jnp.mean(grad_unit * unit_rows, axis=-1, keepdims=True)
    )


def times_transposed(left_side, right_side):
    return lax.dot_general(
        left_side, right_side, (((1,), (1,)), ((), ())), preferred_element_type=jnp.float32
    )


def transposed_times(left_side, right_side):
    return lax.dot_general(
        left_side, right_side, (((0,), (0,)), ((), ())), preferred_element_type=jnp.float32
    )


QUAD = 4


def f32(array):
    return array.astype(jnp.float32)


def bf16(array):
    return array.astype(jnp.bfloat16)


def flip(array, mask):
    return lax.ppermute(array, "dp", [(i, i ^ mask) for i in range(lax.axis_size("dp"))])


def shift(array, step):
    count = lax.axis_size("seq")
    return lax.ppermute(array, "seq", [(i, (i + step) % count) for i in range(count)])


def pair_sum(array):
    count = lax.axis_size("tensor")
    if count != 2:
        return lax.psum(f32(array), "tensor")
    return f32(array) + f32(lax.ppermute(array, "tensor", [(0, 1), (1, 0)]))


def far_groups():
    count = lax.axis_size("dp")
    return [list(range(low, count, QUAD)) for low in range(QUAD)]


def far_gather(array):
    if lax.axis_size("dp") == QUAD:
        return array
    return lax.all_gather(array, "dp", axis=0, tiled=True, axis_index_groups=far_groups())


def far_scatter(array):
    if lax.axis_size("dp") == QUAD:
        return array
    return lax.psum_scatter(
        array, "dp", scatter_dimension=0, tiled=True, axis_index_groups=far_groups()
    )


def mirror(pieces, rank):
    odd, upper = (rank & 1) == 1, (rank & 2) == 2
    a, b, c, d = pieces
    a, b, c, d = (
        jnp.where(odd, b, a),
        jnp.where(odd, a, b),
        jnp.where(odd, d, c),
        jnp.where(odd, c, d),
    )
    return [
        jnp.where(upper, c, a),
        jnp.where(upper, d, b),
        jnp.where(upper, a, c),
        jnp.where(upper, b, d),
    ]


def mirror_columns(array, rank):
    blocks = lax.axis_size("dp")
    width = array.shape[1] // blocks
    cut = [array[:, i * width : (i + 1) * width] for i in range(blocks)]
    moved = []
    for first in range(0, blocks, QUAD):
        moved += mirror(cut[first : first + QUAD], rank)
    return jnp.concatenate(moved, axis=1)


def columns_swapped(array, outer, inner):
    far = lax.axis_size("dp") // QUAD
    width = array.shape[1] // (far * outer * inner)
    cut = []
    for f in range(far):
        for i in range(inner):
            for o in range(outer):
                start = ((f * outer + o) * inner + i) * width
                cut.append(array[:, start : start + width])
    return jnp.concatenate(cut, axis=1)


def quad_pieces(array):
    upper = flip(array, 2)
    return [array, flip(array, 1), upper, flip(upper, 1)]


def quad_sum(pieces):
    near = [
        bf16(f32(pieces[0]) + f32(flip(bf16(pieces[1]), 1))),
        bf16(f32(pieces[2]) + f32(flip(bf16(pieces[3]), 1))),
    ]
    return bf16(f32(near[0]) + f32(flip(near[1], 2)))


def attn_gathered(block):
    far = lax.axis_size("dp") // QUAD
    pieces = quad_pieces(far_gather(lax.all_gather(block, "seq", axis=0, tiled=True)))
    if far == 1:
        return jnp.concatenate(pieces, axis=0)
    cut = [p.reshape(far, -1, p.shape[1]) for p in pieces]
    return jnp.stack(cut, axis=1).reshape(-1, block.shape[1])


def attn_scattered(term):
    far = lax.axis_size("dp") // QUAD
    width = term.shape[1]
    cut = term.reshape(far, QUAD, -1, width)
    near = quad_sum([cut[:, k].reshape(-1, width) for k in range(QUAD)])
    return f32(
        lax.psum_scatter(far_scatter(near), "seq", scatter_dimension=0, tiled=True)
    )


def mlp_gathered(weight, rank):
    rows, columns = weight.shape
    cut = weight.reshape(rows, QUAD, columns // QUAD)
    pieces = []
    for k in range(QUAD):
        part = bf16(lax.dynamic_index_in_dim(cut, rank ^ k, axis=1, keepdims=False))
        pieces.append(flip(part, k) if k else part)
    block = jnp.concatenate(mirror(pieces, rank), axis=0)
    return far_gather(lax.all_gather(block, "seq", axis=0, tiled=True))


def mlp_scattered(term, rank):
    width = term.shape[1]
    own = lax.psum_scatter(
        far_scatter(bf16(term)), "seq", scatter_dimension=0, tiled=True
    ).reshape(QUAD, -1, width)
    pieces = []
    for k in range(QUAD):
        part = lax.dynamic_index_in_dim(own, rank ^ k, axis=0, keepdims=False)
        pieces.append(flip(part, k) if k else part)
    return f32(jnp.concatenate(mirror(pieces, rank), axis=1))


def local(
    tokens,
    out_grad,
    positions,
    attn_gain,
    q_weight,
    k_weight,
    v_weight,
    o_weight,
    mlp_gain,
    gate_weight,
    up_weight,
    down_weight,
):
    seq_count = lax.axis_size("seq")
    seq_rank = lax.axis_index("seq")
    rank = lax.axis_index("dp") % QUAD
    tok_rows, width = tokens.shape
    prompt_rows = PROMPT // seq_count
    cont_here = (tok_rows - prompt_rows) // CONT_LEN

    own_gains = jnp.stack([bf16(attn_gain), bf16(mlp_gain)], axis=1)
    own_gains = jnp.pad(own_gains, ((0, 0), (0, 126)))
    attn_own = jnp.concatenate(
        [bf16(q_weight), bf16(k_weight), bf16(v_weight), own_gains], axis=1
    )
    attn_all = attn_gathered(attn_own)
    o_all = attn_gathered(bf16(o_weight))
    gate_all = mlp_gathered(gate_weight, rank)
    up_all = mlp_gathered(up_weight, rank)
    down_all = mlp_gathered(down_weight, rank)
    q_cols, k_cols = q_weight.shape[1], k_weight.shape[1]
    qkv_cols = q_cols + 2 * k_cols
    qkv_all = attn_all[:, :qkv_cols]
    gains = f32(attn_all[:, qkv_cols:].T)
    gain_one, gain_two = gains[0], gains[1]

    all_pos = positions[0]
    own_pos = lax.dynamic_slice_in_dim(all_pos, seq_rank * tok_rows, tok_rows)
    row_offset = jnp.arange(tok_rows, dtype=jnp.int32)
    cont_number = 1 + seq_rank * cont_here + (row_offset - prompt_rows) // CONT_LEN
    own_seg = jnp.where(row_offset < prompt_rows, jnp.zeros_like(row_offset), cont_number)
    prompt_pos = all_pos.reshape(seq_count, tok_rows)[:, :prompt_rows].reshape(-1)
    prompt_pos = lax.dynamic_slice_in_dim(
        jnp.concatenate([prompt_pos, prompt_pos]), seq_rank * prompt_rows, PROMPT
    )
    key_pos = jnp.concatenate([prompt_pos, own_pos[prompt_rows:]])
    key_seg = jnp.concatenate([jnp.zeros_like(prompt_pos), own_seg[prompt_rows:]])
    visible = (key_pos[None, :] <= own_pos[:, None]) & (
        (key_seg[None, :] == 0) | (key_seg[None, :] == own_seg[:, None])
    )
    angles = (
        own_pos.astype(jnp.float32)[:, None]
        * jnp.asarray(rope_freqs(HEAD_DIM), jnp.float32)[None, :]
    )
    angles = jnp.concatenate([angles, angles], axis=1)
    cos_table = jnp.cos(angles)[:, None, :]
    sin_table = jnp.sin(angles)[:, None, :]
    score_scale = 1.0 / math.sqrt(HEAD_DIM)

    inputs = f32(mirror_columns(tokens, rank))
    grad_out = f32(mirror_columns(out_grad, rank))
    grad_all = jnp.concatenate(
        quad_pieces(columns_swapped(out_grad, QUAD, seq_count)), axis=0
    )
    unit_one, rms_one = norm_parts(inputs)
    normed = bf16(unit_one * gain_one)
    qkv_raw = jnp.dot(normed, qkv_all, preferred_element_type=jnp.float32)
    query_raw = qkv_raw[:, :q_cols]
    key_raw = qkv_raw[:, q_cols : q_cols + k_cols]
    values_own = bf16(qkv_raw[:, q_cols + k_cols :])
    local_heads = q_cols // HEAD_DIM
    local_kv = k_cols // HEAD_DIM
    group_size = local_heads // local_kv
    keys_own = bf16(
        rope_apply(key_raw.reshape(tok_rows, local_kv, HEAD_DIM), cos_table, sin_table)
    ).reshape(tok_rows, -1)
    own_pair = jnp.concatenate([keys_own, values_own], axis=1)
    prompt_pair = [own_pair[:prompt_rows]]
    for step in range(1, seq_count):
        prompt_pair.append(shift(own_pair[:prompt_rows], -step))
    pair_all = jnp.concatenate(prompt_pair + [own_pair[prompt_rows:]], axis=0)
    key_all = pair_all[:, :k_cols].reshape(-1, local_kv, HEAD_DIM)
    value_all = pair_all[:, k_cols:].reshape(-1, local_kv, HEAD_DIM)
    queries = bf16(
        rope_apply(query_raw.reshape(tok_rows, local_heads, HEAD_DIM), cos_table, sin_table)
    )

    def head_scores(query_group, key_group):
        scores = (
            jnp.einsum("tgd,cd->gtc", query_group, key_group, preferred_element_type=jnp.float32)
            * score_scale
        )
        return jnp.where(visible[None], scores, -1e30)

    mixed_list = []
    log_totals = []
    for kv_head in range(local_kv):
        query_group = queries[:, kv_head * group_size : (kv_head + 1) * group_size, :]
        scores = head_scores(query_group, key_all[:, kv_head, :])
        row_max = jnp.max(scores, axis=-1, keepdims=True)
        exponent = jnp.exp(scores - row_max)
        row_total = jnp.sum(exponent, axis=-1, keepdims=True)
        probability = exponent / row_total
        log_totals.append(row_max + jnp.log(row_total))
        mixed_list.append(
            jnp.einsum(
                "gtc,cd->tgd",
                bf16(probability),
                value_all[:, kv_head, :],
                preferred_element_type=jnp.float32,
            )
        )
    attended = bf16(jnp.concatenate(mixed_list, axis=1).reshape(tok_rows, -1))
    middle = inputs + pair_sum(bf16(times_transposed(attended, o_all)))
    unit_two, rms_two = norm_parts(middle)
    normed_two = bf16(unit_two * gain_two)
    normed_all = jnp.concatenate(
        quad_pieces(columns_swapped(mirror_columns(normed_two, rank), QUAD, seq_count)), axis=0
    )
    gate_pre = jnp.dot(normed_all, gate_all, preferred_element_type=jnp.float32)
    upward = jnp.dot(normed_all, up_all, preferred_element_type=jnp.float32)
    sigmoid_gate = jax.nn.sigmoid(gate_pre)
    activated = gate_pre * sigmoid_gate
    hidden = bf16(activated * upward)

    def token_sum(part):
        cut = [part[k * tok_rows : (k + 1) * tok_rows] for k in range(QUAD)]
        total = bf16(pair_sum(quad_sum(cut)))
        return mirror_columns(columns_swapped(total, seq_count, QUAD), rank)

    grad_hidden = jnp.dot(grad_all, down_all, preferred_element_type=jnp.float32)
    grad_gate = bf16(grad_hidden * upward * sigmoid_gate * (1.0 + gate_pre * (1.0 - sigmoid_gate)))
    grad_up = bf16(grad_hidden * activated)
    grad_normed_two = f32(
        token_sum(bf16(times_transposed(grad_gate, gate_all) + times_transposed(grad_up, up_all)))
    )
    down_grad = mlp_scattered(transposed_times(grad_all, hidden), rank)
    gate_grad = mlp_scattered(transposed_times(normed_all, grad_gate), rank)
    up_grad = mlp_scattered(transposed_times(normed_all, grad_up), rank)
    output = mirror_columns(
        bf16(middle + f32(token_sum(bf16(times_transposed(hidden, down_all))))), rank
    )
    grad_middle = grad_out + norm_back(grad_normed_two, unit_two, rms_two, gain_two)
    grad_branch = bf16(grad_middle)
    o_grad = attn_scattered(transposed_times(grad_branch, attended))
    grad_attended = bf16(
        jnp.dot(grad_branch, o_all, preferred_element_type=jnp.float32)
    ).reshape(tok_rows, local_heads, HEAD_DIM)
    query_grads = []
    key_grads = []
    value_grads = []
    for kv_head in range(local_kv):
        query_group = queries[:, kv_head * group_size : (kv_head + 1) * group_size, :]
        key_group = key_all[:, kv_head, :]
        value_group = value_all[:, kv_head, :]
        grad_group = grad_attended[:, kv_head * group_size : (kv_head + 1) * group_size, :]
        probability = jnp.exp(head_scores(query_group, key_group) - log_totals[kv_head])
        grad_prob = jnp.einsum(
            "tgd,cd->gtc", grad_group, value_group, preferred_element_type=jnp.float32
        )
        row_dot = jnp.sum(probability * grad_prob, axis=-1, keepdims=True)
        grad_scores = bf16(probability * (grad_prob - row_dot))
        query_grads.append(
            jnp.einsum("gtc,cd->tgd", grad_scores, key_group, preferred_element_type=jnp.float32)
            * score_scale
        )
        key_grads.append(
            jnp.einsum("gtc,tgd->cd", grad_scores, query_group, preferred_element_type=jnp.float32)
            * score_scale
        )
        value_grads.append(
            jnp.einsum(
                "gtc,tgd->cd",
                bf16(probability),
                grad_group,
                preferred_element_type=jnp.float32,
            )
        )
    grad_queries = jnp.concatenate(query_grads, axis=1)
    grad_keys = jnp.stack(key_grads, axis=1).reshape(-1, local_kv * HEAD_DIM)
    grad_values = jnp.stack(value_grads, axis=1).reshape(-1, local_kv * HEAD_DIM)
    grad_pair = jnp.concatenate([grad_keys, grad_values], axis=1)
    pair_share = grad_pair[:prompt_rows]
    for step in range(1, seq_count):
        part = grad_pair[step * prompt_rows : (step + 1) * prompt_rows]
        pair_share = pair_share + f32(shift(bf16(part), step))
    pair_own = jnp.concatenate([pair_share, grad_pair[PROMPT:]], axis=0)
    grad_query_raw = bf16(rope_back(grad_queries, cos_table, sin_table).reshape(tok_rows, -1))
    grad_key_raw = bf16(
        rope_back(
            pair_own[:, :k_cols].reshape(tok_rows, local_kv, HEAD_DIM), cos_table, sin_table
        ).reshape(tok_rows, -1)
    )
    grad_value_raw = bf16(pair_own[:, k_cols:])
    grad_raw = jnp.concatenate([grad_query_raw, grad_key_raw, grad_value_raw], axis=1)
    qkv_grad = attn_scattered(transposed_times(normed, grad_raw))
    grad_normed = pair_sum(bf16(times_transposed(grad_raw, qkv_all)))
    grad_inputs = grad_middle + norm_back(grad_normed, unit_one, rms_one, gain_one)
    tokens_grad = mirror_columns(bf16(grad_inputs), rank)

    q_grad = qkv_grad[:, :q_cols]
    k_grad = qkv_grad[:, q_cols : q_cols + k_cols]
    v_grad = qkv_grad[:, q_cols + k_cols :]

    def weighed(weight, grad):
        return jnp.sum(f32(bf16(weight)) * grad, axis=1)

    gain_sums = jnp.stack(
        [
            weighed(q_weight, q_grad) + weighed(k_weight, k_grad) + weighed(v_weight, v_grad),
            weighed(gate_weight, gate_grad) + weighed(up_weight, up_grad),
        ]
    )
    gain_sums = pair_sum(gain_sums)
    attn_gain_grad = gain_sums[0] / f32(bf16(attn_gain))
    mlp_gain_grad = gain_sums[1] / f32(bf16(mlp_gain))
    return (
        output,
        tokens_grad,
        attn_gain_grad,
        q_grad,
        k_grad,
        v_grad,
        o_grad,
        mlp_gain_grad,
        gate_grad,
        up_grad,
        down_grad,
    )


def solution(mesh):
    placed = (
        P(("dp", "seq"), None),
        P(("dp", "seq"), None),
        P("dp", None),
        P(("dp", "seq")),
        P(("dp", "seq"), "tensor"),
        P(("dp", "seq"), "tensor"),
        P(("dp", "seq"), "tensor"),
        P(("dp", "seq"), "tensor"),
        P(("dp", "seq")),
        P(("dp", "seq"), "tensor"),
        P(("dp", "seq"), "tensor"),
        P(("dp", "seq"), "tensor"),
    )
    return jax.shard_map(
        local,
        mesh=mesh,
        in_specs=placed,
        out_specs=(
            P(("dp", "seq"), None),
            P(("dp", "seq"), None),
            P(("dp", "seq")),
            P(("dp", "seq"), "tensor"),
            P(("dp", "seq"), "tensor"),
            P(("dp", "seq"), "tensor"),
            P(("dp", "seq"), "tensor"),
            P(("dp", "seq")),
            P(("dp", "seq"), "tensor"),
            P(("dp", "seq"), "tensor"),
            P(("dp", "seq"), "tensor"),
        ),
        check_vma=False,
    )
```
